32 devices in a mesh: groups: 2 (over x), grid: 4 (over y, core), chol: 4 (over z).
Axes of the slice: x: 2, y: 2, z: 4, core: 2. Of those that a mesh axis runs over, the one named last changes fastest.
Arguments:
- chol_block: float32 [8, 1024, 1024], P(('groups', 'chol'), 'grid'), parts along dimension 0, may hold values from -6 to 6
- orbitals: float32 [8192, 1024], P(('groups', 'grid')), parts along dimension 0, may hold values from -0.1875 to 0.1875
- fit_in: float32 [8192, 4096], P(('groups', 'chol'), 'grid'), parts along dimension 0, may hold values from -6 to 6
Outputs:
- fit_out: float32 [8192, 4096], P(('groups', 'chol'), 'grid'), parts along dimension 0
The draws below stay inside these ranges and needn't reach their ends.
There are 2 independent parts, one for each index of `groups`. The reference program is written for one: setup_inputs(seed, part) draws one part's arguments, and reference() takes and returns one part's arrays. A program takes and returns all parts, laid end to end along the dimension named above; each array names one. Nothing has to cross between parts.
All inputs are finite; a program needn't handle non-finite values.
Results may differ from the reference program's by a relative error of at most 0.000096.
Values sent between devices are 32-bit elements; how exact they have to be, the bound alone decides.
A program may use at most 64 MiB of HBM per device.

```python
import jax
import jax.numpy as jnp
from jax import lax

NORB = 1024
NPTS = 4096
NVEC = 4


def levels(own_key, dims, pieces, least, top_value):
    def one(dim, shards_of):
        draws = jax.random.uniform(jax.random.fold_in(jax.random.fold_in(own_key, 6), dim), (shards_of,), jnp.float32, least / len(pieces), top_value / len(pieces))
        return jnp.repeat(jnp.exp(draws), dims[dim] // shards_of).reshape((-1,) + (1,) * (len(dims) - dim - 1))

    factor_of = one(*pieces[0])
    for cut in pieces[1:]:
        factor_of = factor_of * one(*cut)
    return factor_of


def bell_draw(own_key, extent, deviation, limit, split=(), kind=jnp.bfloat16):
    loudness = levels(own_key, extent, split, -0.22, 0.18) if split else 1.0
    result = jax.random.normal(own_key, extent, jnp.float32) * deviation * loudness
    return jnp.minimum(jnp.maximum(result, -limit), limit).astype(kind)


def setup_inputs(seed: int = 0, part: int = 0) -> dict:
    splits = jax.random.split(jax.random.key(seed), 4)
    part_keys = jax.random.split(jax.random.fold_in(splits[3], part), 4)
    chol_block = bell_draw(part_keys[0], (NVEC, NORB, NORB), 1.0, 6.0, ((0, 4), (1, 4)), jnp.float32)
    orbitals = bell_draw(part_keys[1], (NPTS, NORB), NORB ** -0.5, 0.1875, ((0, 4),), jnp.float32)
    fit_in = bell_draw(part_keys[2], (NPTS, NPTS), 1.0, 6.0, ((0, 4), (1, 4)), jnp.float32)
    return {"chol_block": chol_block, "orbitals": orbitals, "fit_in": fit_in}


def one_vector(factor, orbitals):
    halfway = jnp.dot(orbitals, factor, precision=lax.Precision.HIGHEST)
    return jnp.sum(halfway * orbitals, axis=1)


def reference(chol_block, orbitals, fit_in):
    columns = lax.map(lambda factor: one_vector(factor, orbitals), chol_block)
    contracted = jnp.transpose(columns)
    product = jnp.dot(contracted, jnp.transpose(contracted), precision=lax.Precision.HIGHEST)
    return fit_in + product
```

```python
import functools

import jax
import jax.numpy as jnp
from jax import lax
from jax.experimental import pallas as pl
from jax.experimental.pallas import tpu as pltpu
from jax.sharding import PartitionSpec as P

MESH = pl.DeviceIdType.MESH
F32 = jnp.float32
BF16 = jnp.bfloat16


def split2(a):
    hi = a.astype(BF16)
    return hi, (a - hi.astype(F32)).astype(BF16)


def dot(a, b):
    return jnp.dot(a, b, preferred_element_type=F32)


def gather_kernel(ng, nc, nch, chol_hbm, orb_hbm, lhs_ref, rhs_ref,
                  lbuf, xbuf, xt, xth, xtl, acc, allc,
                  own_sem, x_sem, ysend, yrecv, ssend, srecv, csend, crecv):
    g = lax.axis_index("groups")
    i = lax.axis_index("grid")
    c = lax.axis_index("chol")
    rows, norb = lbuf.shape[1], lbuf.shape[2]
    pts = allc.shape[2]
    total = ng * nc
    chips = ng // 2
    core = lax.rem(i, 2)
    chip = lax.div(i, 2)
    sib = i + 1 - 2 * core
    flat = i * nc + c
    step = rows // nch

    own = pltpu.make_async_copy(chol_hbm.at[0], lbuf.at[i], own_sem)
    own.start()
    xcopy = pltpu.make_async_copy(orb_hbm, xbuf, x_sem)
    xcopy.start()

    barrier = pltpu.get_barrier_semaphore()
    for k in range(1, total):
        t = lax.rem(flat + k, total)
        pl.semaphore_signal(barrier, inc=1, device_id=(g, lax.div(t, nc), lax.rem(t, nc)), device_id_type=MESH)
    pl.semaphore_wait(barrier, total - 1)

    def chip_copy(ch, d):
        part = pl.ds(ch * step, step)
        to = lax.rem(chip + d, chips) * 2 + core
        return pltpu.make_async_remote_copy(
            src_ref=chol_hbm.at[0, part], dst_ref=lbuf.at[i, part],
            send_sem=ysend.at[ch, d], recv_sem=yrecv.at[ch, d],
            device_id=(g, to, c), device_id_type=MESH)

    def from_chip(ch, d):
        part = pl.ds(ch * step, step)
        src = lax.rem(chip - d + chips, chips) * 2 + core
        return src, pltpu.make_async_remote_copy(
            src_ref=lbuf.at[src, part], dst_ref=lbuf.at[src, part],
            send_sem=ysend.at[ch, d], recv_sem=yrecv.at[ch, d],
            device_id=(g, src, c), device_id_type=MESH)

    def forward(ch, d, src):
        part = pl.ds(ch * step, step)
        return pltpu.make_async_remote_copy(
            src_ref=lbuf.at[src, part], dst_ref=lbuf.at[src, part],
            send_sem=ssend.at[ch, d], recv_sem=srecv.at[ch, d],
            device_id=(g, sib, c), device_id_type=MESH)

    for ch in range(nch):
        for d in range(1, chips):
            chip_copy(ch, d).start()
    home = pltpu.make_async_remote_copy(
        src_ref=chol_hbm.at[0], dst_ref=lbuf.at[i],
        send_sem=ssend.at[0, 0], recv_sem=srecv.at[0, 0],
        device_id=(g, sib, c), device_id_type=MESH)
    home.start()

    xcopy.wait()
    tile = min(256, pts)

    @pl.loop(0, pts // tile)
    def _(p):
        at = pl.multiple_of(p * tile, tile)
        block = jnp.transpose(xbuf[pl.ds(at, tile), :])
        xt[:, pl.ds(at, tile)] = block
        hi, lo = split2(block)
        xth[:, pl.ds(at, tile)] = hi
        xtl[:, pl.ds(at, tile)] = lo

    acc[...] = jnp.zeros_like(acc)

    def add(src, first, count):
        hi, lo = split2(lbuf[src, pl.ds(first, count), :])
        base = pl.multiple_of(src * rows + first, 16)

        @pl.loop(0, pts // tile)
        def _(p):
            at = pl.multiple_of(p * tile, tile)
            cols = pl.ds(at, tile)
            half = dot(hi, xth[:, cols]) + (dot(lo, xth[:, cols]) + dot(hi, xtl[:, cols]))
            prod = half * xt[pl.ds(base, count), cols]
            acc[:, cols] += jnp.sum(prod.reshape(count // 8, 8, tile), axis=0)

    own.wait()
    add(i, 0, rows)
    home.wait()
    add(sib, 0, rows)

    for ch in range(nch):
        for d in range(1, chips):
            src, landed = from_chip(ch, d)
            landed.wait_recv()
            fwd = forward(ch, d, src)
            fwd.start()
            add(src, ch * step, step)
            fwd.wait_recv()
            add(src + 1 - 2 * core, ch * step, step)

    allc[flat] = jnp.sum(acc[...], axis=0, keepdims=True)

    def spread(k):
        t = lax.rem(flat + k, total)
        return pltpu.make_async_remote_copy(
            src_ref=allc.at[flat], dst_ref=allc.at[flat],
            send_sem=csend.at[k], recv_sem=crecv.at[k],
            device_id=(g, lax.div(t, nc), lax.rem(t, nc)), device_id_type=MESH)

    for k in range(1, total):
        spread(k).start()
    for ch in range(nch):
        for d in range(1, chips):
            src, _ = from_chip(ch, d)
            chip_copy(ch, d).wait_send()
            forward(ch, d, src).wait_send()
    for k in range(1, total):
        back = lax.rem(flat - k + total, total)
        pltpu.make_async_remote_copy(
            src_ref=allc.at[back], dst_ref=allc.at[back],
            send_sem=csend.at[k], recv_sem=crecv.at[k],
            device_id=(g, i, c), device_id_type=MESH).wait_recv()

    def terms(v):
        h = v.astype(BF16).astype(F32)
        r = v - h
        m = r.astype(BF16).astype(F32)
        return h, m, (r - m).astype(BF16).astype(F32)

    lhs_ref[...] = jnp.zeros_like(lhs_ref)
    rhs_ref[...] = jnp.zeros_like(rhs_ref)
    blocks = lhs_ref.shape[1] // pts
    for n in range(nc):
        h, m, l = terms(allc[i * nc + n])
        for t, v in enumerate((h, m, h, l, h, m)):
            rhs_ref[t * nc + n:t * nc + n + 1, :] = v
        for b in range(blocks):
            h, m, l = terms(allc[(c * blocks + b) * nc + n])
            for t, v in enumerate((h, h, m, h, l, m)):
                lhs_ref[t * nc + n:t * nc + n + 1, b * pts:(b + 1) * pts] = v
    for k in range(1, total):
        spread(k).wait_send()


def fit_kernel(lhs_ref, rhs_ref, fit_ref, out_ref):
    left = jnp.transpose(lhs_ref[...]).astype(BF16)
    out_ref[...] = fit_ref[...] + dot(left, rhs_ref[...].astype(BF16))


def on_device(ng, nc, chol_block, orbitals, fit_in):
    rows, norb = chol_block.shape[1:]
    pts = orbitals.shape[0]
    tile_rows, tile_cols = fit_in.shape
    nch = 4
    chips = ng // 2
    depth = -(-6 * nc // 8) * 8
    total = ng * nc
    dma = pltpu.SemaphoreType.DMA
    vmem = pl.BlockSpec(memory_space=pltpu.VMEM)
    hbm = pl.BlockSpec(memory_space=pl.ANY)
    lhs, rhs = pl.pallas_call(
        functools.partial(gather_kernel, ng, nc, nch),
        out_shape=(jax.ShapeDtypeStruct((depth, tile_rows), F32),
                   jax.ShapeDtypeStruct((depth, tile_cols), F32)),
        in_specs=[hbm, hbm],
        out_specs=(vmem, vmem),
        scratch_shapes=[
            pltpu.VMEM((ng, rows, norb), F32),
            pltpu.VMEM((pts, norb), F32),
            pltpu.VMEM((norb, pts), F32),
            pltpu.VMEM((norb, pts), BF16),
            pltpu.VMEM((norb, pts), BF16),
            pltpu.VMEM((8, pts), F32),
            pltpu.VMEM((total, 1, pts), F32),
            dma, dma,
            dma((nch, chips)), dma((nch, chips)),
            dma((nch, chips)), dma((nch, chips)),
            dma((total,)), dma((total,)),
        ],
        compiler_params=pltpu.CompilerParams(
            collective_id=0, has_side_effects=True, vmem_limit_bytes=40 << 20),
        name="gather",
    )(chol_block, orbitals)
    tile = min(256, tile_rows)
    return pl.pallas_call(
        fit_kernel,
        grid=(tile_rows // tile,),
        out_shape=jax.ShapeDtypeStruct(fit_in.shape, F32),
        in_specs=[
            pl.BlockSpec((depth, tile), lambda r: (0, r)),
            pl.BlockSpec((depth, tile_cols), lambda r: (0, 0)),
            pl.BlockSpec((tile, tile_cols), lambda r: (r, 0)),
        ],
        out_specs=pl.BlockSpec((tile, tile_cols), lambda r: (r, 0)),
        name="fit",
    )(lhs, rhs, fit_in)


def solution(mesh):
    placed = (
        P(("groups", "chol"), "grid", None),
        P(("groups", "grid"), None),
        P(("groups", "chol"), "grid"),
    )
    return jax.shard_map(
        functools.partial(on_device, mesh.shape["grid"], mesh.shape["chol"]),
        mesh=mesh,
        in_specs=placed,
        out_specs=P(("groups", "chol"), "grid"),
        check_vma=False,
    )
```

```python
import functools

import jax
import jax.numpy as jnp
from jax import lax
from jax.experimental import pallas as pl
from jax.experimental.pallas import tpu as pltpu
from jax.sharding import PartitionSpec as P

MESH = pl.DeviceIdType.MESH
F32 = jnp.float32
BF16 = jnp.bfloat16


def split2(a):
    hi = a.astype(BF16)
    return hi, (a - hi.astype(F32)).astype(BF16)


def dot(a, b):
    return jnp.dot(a, b, preferred_element_type=F32)


def gather_kernel(ng, nc, nch, chol_hbm, orb_hbm, fit_hbm, lhs_ref, rhs_ref, held_ref,
                  lbuf, xbuf, xt, xth, xtl, acc, allc,
                  own_sem, x_sem, fit_sem, ysend, yrecv, ssend, srecv, csend, crecv):
    g = lax.axis_index("groups")
    i = lax.axis_index("grid")
    c = lax.axis_index("chol")
    rows, norb = lbuf.shape[1], lbuf.shape[2]
    pts = allc.shape[2]
    total = ng * nc
    chips = ng // 2
    core = lax.rem(i, 2)
    chip = lax.div(i, 2)
    sib = i + 1 - 2 * core
    flat = i * nc + c
    step = rows // nch

    own = pltpu.make_async_copy(chol_hbm.at[0], lbuf.at[i], own_sem)
    own.start()
    xcopy = pltpu.make_async_copy(orb_hbm, xbuf, x_sem)
    xcopy.start()

    barrier = pltpu.get_barrier_semaphore()
    for k in range(1, total):
        t = lax.rem(flat + k, total)
        pl.semaphore_signal(barrier, inc=1, device_id=(g, lax.div(t, nc), lax.rem(t, nc)), device_id_type=MESH)
    pl.semaphore_wait(barrier, total - 1)

    def chip_copy(ch, d):
        part = pl.ds(ch * step, step)
        to = lax.rem(chip + d, chips) * 2 + core
        return pltpu.make_async_remote_copy(
            src_ref=chol_hbm.at[0, part], dst_ref=lbuf.at[i, part],
            send_sem=ysend.at[ch, d], recv_sem=yrecv.at[ch, d],
            device_id=(g, to, c), device_id_type=MESH)

    def from_chip(ch, d):
        part = pl.ds(ch * step, step)
        src = lax.rem(chip - d + chips, chips) * 2 + core
        return src, pltpu.make_async_remote_copy(
            src_ref=lbuf.at[src, part], dst_ref=lbuf.at[src, part],
            send_sem=ysend.at[ch, d], recv_sem=yrecv.at[ch, d],
            device_id=(g, src, c), device_id_type=MESH)

    def forward(ch, d, src):
        part = pl.ds(ch * step, step)
        return pltpu.make_async_remote_copy(
            src_ref=lbuf.at[src, part], dst_ref=lbuf.at[src, part],
            send_sem=ssend.at[ch, d], recv_sem=srecv.at[ch, d],
            device_id=(g, sib, c), device_id_type=MESH)

    for ch in range(nch):
        for d in range(1, chips):
            chip_copy(ch, d).start()
    home = pltpu.make_async_remote_copy(
        src_ref=chol_hbm.at[0], dst_ref=lbuf.at[i],
        send_sem=ssend.at[0, 0], recv_sem=srecv.at[0, 0],
        device_id=(g, sib, c), device_id_type=MESH)
    home.start()

    xcopy.wait()
    keep = pltpu.make_async_copy(fit_hbm, held_ref, fit_sem)
    keep.start()
    tile = min(256, pts)

    @pl.loop(0, pts // tile)
    def _(p):
        at = pl.multiple_of(p * tile, tile)
        block = jnp.transpose(xbuf[pl.ds(at, tile), :])
        xt[:, pl.ds(at, tile)] = block
        hi, lo = split2(block)
        xth[:, pl.ds(at, tile)] = hi
        xtl[:, pl.ds(at, tile)] = lo

    acc[...] = jnp.zeros_like(acc)

    def add(src, first, count):
        hi, lo = split2(lbuf[src, pl.ds(first, count), :])
        base = pl.multiple_of(src * rows + first, 16)

        @pl.loop(0, pts // tile)
        def _(p):
            at = pl.multiple_of(p * tile, tile)
            cols = pl.ds(at, tile)
            half = dot(hi, xth[:, cols]) + (dot(lo, xth[:, cols]) + dot(hi, xtl[:, cols]))
            prod = half * xt[pl.ds(base, count), cols]
            acc[:, cols] += jnp.sum(prod.reshape(count // 8, 8, tile), axis=0)

    own.wait()
    add(i, 0, rows)
    home.wait()
    add(sib, 0, rows)

    for ch in range(nch):
        for d in range(1, chips):
            src, landed = from_chip(ch, d)
            landed.wait_recv()
            fwd = forward(ch, d, src)
            fwd.start()
            add(src, ch * step, step)
            fwd.wait_recv()
            add(src + 1 - 2 * core, ch * step, step)

    allc[flat] = jnp.sum(acc[...], axis=0, keepdims=True)

    def spread(k):
        t = lax.rem(flat + k, total)
        return pltpu.make_async_remote_copy(
            src_ref=allc.at[flat], dst_ref=allc.at[flat],
            send_sem=csend.at[k], recv_sem=crecv.at[k],
            device_id=(g, lax.div(t, nc), lax.rem(t, nc)), device_id_type=MESH)

    for k in range(1, total):
        spread(k).start()
    for ch in range(nch):
        for d in range(1, chips):
            src, _ = from_chip(ch, d)
            chip_copy(ch, d).wait_send()
            forward(ch, d, src).wait_send()
    for k in range(1, total):
        back = lax.rem(flat - k + total, total)
        pltpu.make_async_remote_copy(
            src_ref=allc.at[back], dst_ref=allc.at[back],
            send_sem=csend.at[k], recv_sem=crecv.at[k],
            device_id=(g, i, c), device_id_type=MESH).wait_recv()

    def terms(v):
        h = v.astype(BF16).astype(F32)
        r = v - h
        m = r.astype(BF16).astype(F32)
        return h, m, (r - m).astype(BF16).astype(F32)

    lhs_ref[...] = jnp.zeros_like(lhs_ref)
    rhs_ref[...] = jnp.zeros_like(rhs_ref)
    blocks = lhs_ref.shape[1] // pts
    for n in range(nc):
        h, m, l = terms(allc[i * nc + n])
        for t, v in enumerate((h, m, h, l, h, m)):
            rhs_ref[t * nc + n:t * nc + n + 1, :] = v
        for b in range(blocks):
            h, m, l = terms(allc[(c * blocks + b) * nc + n])
            for t, v in enumerate((h, h, m, h, l, m)):
                lhs_ref[t * nc + n:t * nc + n + 1, b * pts:(b + 1) * pts] = v
    for k in range(1, total):
        spread(k).wait_send()
    keep.wait()


def fit_kernel(pieces, lhs_ref, rhs_ref, held_ref, out_hbm, obuf, sems):
    left = jnp.transpose(lhs_ref[...]).astype(BF16)
    right = rhs_ref[...].astype(BF16)
    step = obuf.shape[0] // pieces
    copies = []
    for p in range(pieces):
        part = pl.ds(p * step, step)
        obuf[part, :] = held_ref[part, :] + dot(left[p * step:(p + 1) * step], right)
        copies.append(pltpu.make_async_copy(obuf.at[part], out_hbm.at[part], sems.at[p]))
        copies[-1].start()
    for copy in copies:
        copy.wait()


def on_device(ng, nc, chol_block, orbitals, fit_in):
    rows, norb = chol_block.shape[1:]
    pts = orbitals.shape[0]
    tile_rows, tile_cols = fit_in.shape
    nch = 4
    chips = ng // 2
    depth = -(-6 * nc // 8) * 8
    total = ng * nc
    dma = pltpu.SemaphoreType.DMA
    vmem = pl.BlockSpec(memory_space=pltpu.VMEM)
    hbm = pl.BlockSpec(memory_space=pltpu.HBM)
    lhs, rhs, held = pl.pallas_call(
        functools.partial(gather_kernel, ng, nc, nch),
        out_shape=(jax.ShapeDtypeStruct((depth, tile_rows), F32),
                   jax.ShapeDtypeStruct((depth, tile_cols), F32),
                   jax.ShapeDtypeStruct(fit_in.shape, F32)),
        in_specs=[hbm, hbm, hbm],
        out_specs=(vmem, vmem, vmem),
        scratch_shapes=[
            pltpu.VMEM((ng, rows, norb), F32),
            pltpu.VMEM((pts, norb), F32),
            pltpu.VMEM((norb, pts), F32),
            pltpu.VMEM((norb, pts), BF16),
            pltpu.VMEM((norb, pts), BF16),
            pltpu.VMEM((8, pts), F32),
            pltpu.VMEM((total, 1, pts), F32),
            dma, dma, dma,
            dma((nch, chips)), dma((nch, chips)),
            dma((nch, chips)), dma((nch, chips)),
            dma((total,)), dma((total,)),
        ],
        compiler_params=pltpu.CompilerParams(
            collective_id=0, has_side_effects=True, vmem_limit_bytes=40 << 20),
        name="gather",
    )(*(pltpu.with_memory_space_constraint(a, pltpu.HBM) for a in (chol_block, orbitals, fit_in)))
    pieces = 8
    return pl.pallas_call(
        functools.partial(fit_kernel, pieces),
        out_shape=jax.ShapeDtypeStruct(fit_in.shape, F32),
        in_specs=[vmem, vmem, vmem],
        out_specs=hbm,
        scratch_shapes=[pltpu.VMEM(fit_in.shape, F32), dma((pieces,))],
        compiler_params=pltpu.CompilerParams(vmem_limit_bytes=20 << 20),
        name="fit",
    )(lhs, rhs, held)


def solution(mesh):
    placed = (
        P(("groups", "chol"), "grid", None),
        P(("groups", "grid"), None),
        P(("groups", "chol"), "grid"),
    )
    return jax.shard_map(
        functools.partial(on_device, mesh.shape["grid"], mesh.shape["chol"]),
        mesh=mesh,
        in_specs=placed,
        out_specs=P(("groups", "chol"), "grid"),
        check_vma=False,
    )
```

```python
import functools

import jax
import jax.numpy as jnp
from jax import lax
from jax.experimental import pallas as pl
from jax.experimental.pallas import tpu as pltpu
from jax.sharding import PartitionSpec as P

MESH = pl.DeviceIdType.MESH
F32 = jnp.float32
BF16 = jnp.bfloat16


def split2(a):
    hi = a.astype(BF16)
    return hi, (a - hi.astype(F32)).astype(BF16)


def dot(a, b):
    return jnp.dot(a, b, preferred_element_type=F32)


TILE = 256


class Place:
    def __init__(self, ng, nc):
        self.ng, self.nc, self.total, self.chips = ng, nc, ng * nc, ng // 2
        self.g = lax.axis_index("groups")
        self.i = lax.axis_index("grid")
        self.c = lax.axis_index("chol")
        self.core = lax.rem(self.i, 2)
        self.chip = lax.div(self.i, 2)
        self.sib = self.i + 1 - 2 * self.core
        self.flat = self.i * nc + self.c

    def peer(self, k):
        t = lax.rem(self.flat + k, self.total)
        return (self.g, lax.div(t, self.nc), lax.rem(t, self.nc))

    def greet(self):
        barrier = pltpu.get_barrier_semaphore()
        for k in range(1, self.total):
            pl.semaphore_signal(barrier, inc=1, device_id=self.peer(k), device_id_type=MESH)
        pl.semaphore_wait(barrier, self.total - 1)

    def send(self, src, dst, send_sem, recv_sem, to):
        return pltpu.make_async_remote_copy(
            src_ref=src, dst_ref=dst, send_sem=send_sem, recv_sem=recv_sem,
            device_id=(self.g, to, self.c), device_id_type=MESH)


def turn(xbuf, xt, xth, xtl):
    pts = xbuf.shape[0]
    tile = min(256, pts)

    @pl.loop(0, pts // tile)
    def _(p):
        at = pl.multiple_of(p * tile, tile)
        block = jnp.transpose(xbuf[pl.ds(at, tile), :])
        xt[:, pl.ds(at, tile)] = block
        hi, lo = split2(block)
        xth[:, pl.ds(at, tile)] = hi
        xtl[:, pl.ds(at, tile)] = lo


def add(acc, xt, xth, xtl, block, base, spans):
    count = block.shape[0]
    pts = xt.shape[1]
    tile = min(TILE, pts)
    hi, lo = split2(block)
    both = jnp.concatenate([hi, lo], axis=0)

    @pl.loop(0, pts // tile)
    def _(p):
        at = pl.multiple_of(p * tile, tile)
        cols = pl.ds(at, tile)
        half = None
        for first, where, width in spans:
            k = pl.ds(pl.multiple_of(where, 16), width)
            two = dot(both[:, first:first + width], xth[k, cols])
            term = two[:count] + (two[count:] + dot(hi[:, first:first + width], xtl[k, cols]))
            half = term if half is None else half + term
        prod = half * xt[pl.ds(pl.multiple_of(base, 8), count), cols]
        acc[:, cols] += jnp.sum(prod.reshape(count // 8, 8, tile), axis=0)


def finish(at, acc, allc, lhs_ref, rhs_ref, csend, crecv, drain):
    nc, total, pts = at.nc, at.total, allc.shape[2]
    allc[at.flat] = jnp.sum(acc[...], axis=0, keepdims=True)

    def spread(k):
        return pltpu.make_async_remote_copy(
            src_ref=allc.at[at.flat], dst_ref=allc.at[at.flat],
            send_sem=csend.at[k], recv_sem=crecv.at[k],
            device_id=at.peer(k), device_id_type=MESH)

    for k in range(1, total):
        spread(k).start()
    lhs_ref[...] = jnp.zeros_like(lhs_ref)
    rhs_ref[...] = jnp.zeros_like(rhs_ref)
    drain()
    for k in range(1, total):
        back = lax.rem(at.flat - k + total, total)
        pltpu.make_async_remote_copy(
            src_ref=allc.at[back], dst_ref=allc.at[back],
            send_sem=csend.at[k], recv_sem=crecv.at[k],
            device_id=(at.g, at.i, at.c), device_id_type=MESH).wait_recv()

    def terms(v):
        h = v.astype(BF16).astype(F32)
        r = v - h
        m = r.astype(BF16).astype(F32)
        return h, m, (r - m).astype(BF16).astype(F32)

    blocks = lhs_ref.shape[1] // pts
    for n in range(nc):
        h, m, l = terms(allc[at.i * nc + n])
        for t, v in enumerate((h, m, h, l, h, m)):
            rhs_ref[t * nc + n:t * nc + n + 1, :] = v
        for b in range(blocks):
            h, m, l = terms(allc[(at.c * blocks + b) * nc + n])
            for t, v in enumerate((h, h, m, h, l, m)):
                lhs_ref[t * nc + n:t * nc + n + 1, b * pts:(b + 1) * pts] = v
    for k in range(1, total):
        spread(k).wait_send()


def begin(at, chol_hbm, orb_hbm, fit_hbm, held_ref, mine, xbuf, sems):
    copies = [pltpu.make_async_copy(chol_hbm.at[0], mine, sems.at[0]),
              pltpu.make_async_copy(orb_hbm, xbuf, sems.at[1]),
              pltpu.make_async_copy(fit_hbm, held_ref, sems.at[2])]
    copies[0].start()
    copies[1].start()
    at.greet()
    return copies


def pair_kernel(ng, nc, nch, chol_hbm, orb_hbm, fit_hbm, lhs_ref, rhs_ref, held_ref,
                lbuf, obuf, dsend, esend, dbuf, ebuf, xbuf, xt, xth, xtl, acc, allc,
                sems, ysend, yrecv, ssend, srecv, csend, crecv):
    at = Place(ng, nc)
    rows = lbuf.shape[1]
    half, step, wide = rows // 2, rows // nch, 2 * rows
    core, other = at.core, 1 - at.core
    away = (1 - at.chip) * 2 + core
    pieces = nch + 2
    own, xcopy, keep = begin(at, chol_hbm, orb_hbm, fit_hbm, held_ref, lbuf.at[core], xbuf, sems)
    far = pl.ds(pl.multiple_of((1 - at.chip) * wide, 128), wide)

    def slot(p, s):
        if p < nch:
            return obuf.at[s, pl.ds(p * step, step)]
        return (dbuf if p == nch else ebuf).at[s]

    def over(p):
        if p < nch:
            src = chol_hbm.at[0, pl.ds(p * step, step), far]
        else:
            src = dsend if p == nch else esend
        return at.send(src, slot(p, core), ysend.at[p], yrecv.at[p], away)

    def forward(p):
        return at.send(slot(p, core), slot(p, core), ssend.at[p], srecv.at[p], at.sib)

    for p in range(nch):
        over(p).start()
    home = at.send(chol_hbm.at[0], lbuf.at[core], ssend.at[pieces], srecv.at[pieces], at.sib)
    home.start()
    xcopy.wait()
    turn(xbuf, xt, xth, xtl)
    acc[...] = jnp.zeros_like(acc)

    own.wait()
    home.wait_recv()
    mine = pl.multiple_of(at.i * rows, 128)
    theirs = pl.multiple_of(at.sib * rows, 128)

    def both_ways(h):
        k = core + h - 2 * core * h
        one = lbuf[core, h * half:(h + 1) * half, pl.ds(pl.multiple_of(theirs + k * half, 128), half)]
        two = lbuf[other, pl.ds(pl.multiple_of(k * half, 8), half), pl.ds(pl.multiple_of(mine + h * half, 128), half)]
        return one + jnp.transpose(two)

    left = pl.ds(mine, half)
    right = pl.ds(pl.multiple_of(mine + half, 128), half)
    dsend[:, :half] = lbuf[core, :half, left]
    dsend[:, half:2 * half] = lbuf[core, :half, right] + jnp.transpose(lbuf[core, half:, left])
    dsend[:, 2 * half:] = both_ways(0)
    esend[:, :half] = lbuf[core, half:, right]
    esend[:, half:] = both_ways(1)
    over(nch).start()
    over(nch + 1).start()
    keep.start()

    put = functools.partial(add, acc, xt, xth, xtl)
    norb = lbuf.shape[2]
    put(lbuf[core], mine, [(0, 0, norb)])
    put(lbuf[other], theirs, [(0, 0, norb)])

    def take(p, s):
        src = ((1 - at.chip) * 2 + s) * rows
        sib = ((1 - at.chip) * 2 + 1 - s) * rows
        if p < nch:
            put(obuf[s, p * step:(p + 1) * step], src + p * step, [(0, at.chip * wide, wide)])
        elif p == nch:
            put(dbuf[s], src, [(0, src, 2 * half), (2 * half, sib + s * half, half)])
        else:
            put(ebuf[s], src + half, [(0, src + half, half), (half, sib + (1 - s) * half, half)])

    for p in range(pieces):
        over(p).wait_recv()
        forward(p).start()
        take(p, core)
        forward(p).wait_recv()
        take(p, other)

    def drain():
        home.wait_send()
        for p in range(pieces):
            over(p).wait_send()
            forward(p).wait_send()
        keep.wait()

    finish(at, acc, allc, lhs_ref, rhs_ref, csend, crecv, drain)


def ring_kernel(ng, nc, nch, chol_hbm, orb_hbm, fit_hbm, lhs_ref, rhs_ref, held_ref,
                lbuf, xbuf, xt, xth, xtl, acc, allc,
                sems, ysend, yrecv, ssend, srecv, csend, crecv):
    at = Place(ng, nc)
    rows, norb = lbuf.shape[1:]
    step = rows // nch
    own, xcopy, keep = begin(at, chol_hbm, orb_hbm, fit_hbm, held_ref, lbuf.at[at.i], xbuf, sems)

    def over(ch, d):
        part = pl.ds(ch * step, step)
        to = lax.rem(at.chip + d, at.chips) * 2 + at.core
        return at.send(chol_hbm.at[0, part], lbuf.at[at.i, part], ysend.at[ch, d], yrecv.at[ch, d], to)

    def source(d):
        return lax.rem(at.chip - d + at.chips, at.chips) * 2 + at.core

    def forward(ch, d):
        ref = lbuf.at[source(d), pl.ds(ch * step, step)]
        return at.send(ref, ref, ssend.at[ch, d], srecv.at[ch, d], at.sib)

    for ch in range(nch):
        for d in range(1, at.chips):
            over(ch, d).start()
    home = at.send(chol_hbm.at[0], lbuf.at[at.i], ssend.at[0, 0], srecv.at[0, 0], at.sib)
    home.start()
    keep.start()
    xcopy.wait()
    turn(xbuf, xt, xth, xtl)
    acc[...] = jnp.zeros_like(acc)

    def put(src, first, count):
        add(acc, xt, xth, xtl, lbuf[src, pl.ds(first, count), :], src * rows + first, [(0, 0, norb)])

    own.wait()
    put(at.i, 0, rows)
    home.wait()
    put(at.sib, 0, rows)
    for ch in range(nch):
        for d in range(1, at.chips):
            src = source(d)
            over(ch, d).wait_recv()
            forward(ch, d).start()
            put(src, ch * step, step)
            forward(ch, d).wait_recv()
            put(src + 1 - 2 * at.core, ch * step, step)

    def drain():
        for ch in range(nch):
            for d in range(1, at.chips):
                over(ch, d).wait_send()
                forward(ch, d).wait_send()
        keep.wait()

    finish(at, acc, allc, lhs_ref, rhs_ref, csend, crecv, drain)


def fit_kernel(pieces, lhs_ref, rhs_ref, held_ref, out_hbm, obuf, sems):
    left = jnp.transpose(lhs_ref[...]).astype(BF16)
    right = rhs_ref[...].astype(BF16)
    step = obuf.shape[0] // pieces
    copies = []
    for p in range(pieces):
        part = pl.ds(p * step, step)
        obuf[part, :] = held_ref[part, :] + dot(left[p * step:(p + 1) * step], right)
        copies.append(pltpu.make_async_copy(obuf.at[part], out_hbm.at[part], sems.at[p]))
        copies[-1].start()
    for copy in copies:
        copy.wait()


def on_device(ng, nc, chol_block, orbitals, fit_in):
    rows, norb = chol_block.shape[1:]
    pts = orbitals.shape[0]
    tile_rows, tile_cols = fit_in.shape
    chips = ng // 2
    depth = -(-6 * nc // 8) * 8
    total = ng * nc
    dma = pltpu.SemaphoreType.DMA
    vmem = pl.BlockSpec(memory_space=pltpu.VMEM)
    hbm = pl.BlockSpec(memory_space=pltpu.HBM)
    if chips == 2 and rows % 256 == 0:
        kernel, nch, half = pair_kernel, 2, rows // 2
        blocks = [(2, rows, norb), (2, rows, 2 * rows), (half, 3 * half), (half, 2 * half),
                  (2, half, 3 * half), (2, half, 2 * half)]
        links = [dma((nch + 2,)), dma((nch + 2,)), dma((nch + 3,)), dma((nch + 3,))]
    else:
        kernel, nch = ring_kernel, 4
        blocks = [(ng, rows, norb)]
        links = [dma((nch, chips))] * 4
    lhs, rhs, held = pl.pallas_call(
        functools.partial(kernel, ng, nc, nch),
        out_shape=(jax.ShapeDtypeStruct((depth, tile_rows), F32),
                   jax.ShapeDtypeStruct((depth, tile_cols), F32),
                   jax.ShapeDtypeStruct(fit_in.shape, F32)),
        in_specs=[hbm, hbm, hbm],
        out_specs=(vmem, vmem, vmem),
        scratch_shapes=[
            *(pltpu.VMEM(shape, F32) for shape in blocks),
            pltpu.VMEM((pts, norb), F32),
            pltpu.VMEM((norb, pts), F32),
            pltpu.VMEM((norb, pts), BF16),
            pltpu.VMEM((norb, pts), BF16),
            pltpu.VMEM((8, pts), F32),
            pltpu.VMEM((total, 1, pts), F32),
            dma((3,)), *links,
            dma((total,)), dma((total,)),
        ],
        compiler_params=pltpu.CompilerParams(
            collective_id=0, has_side_effects=True, vmem_limit_bytes=40 << 20),
        name="gather",
    )(*(pltpu.with_memory_space_constraint(a, pltpu.HBM) for a in (chol_block, orbitals, fit_in)))
    pieces = 8
    return pl.pallas_call(
        functools.partial(fit_kernel, pieces),
        out_shape=jax.ShapeDtypeStruct(fit_in.shape, F32),
        in_specs=[vmem, vmem, vmem],
        out_specs=hbm,
        scratch_shapes=[pltpu.VMEM(fit_in.shape, F32), dma((pieces,))],
        compiler_params=pltpu.CompilerParams(vmem_limit_bytes=20 << 20),
        name="fit",
    )(lhs, rhs, held)


def solution(mesh):
    placed = (
        P(("groups", "chol"), "grid", None),
        P(("groups", "grid"), None),
        P(("groups", "chol"), "grid"),
    )
    return jax.shard_map(
        functools.partial(on_device, mesh.shape["grid"], mesh.shape["chol"]),
        mesh=mesh,
        in_specs=placed,
        out_specs=P(("groups", "chol"), "grid"),
        check_vma=False,
    )
```

```python
import functools

import jax
import jax.numpy as jnp
from jax import lax
from jax.experimental import pallas as pl
from jax.experimental.pallas import tpu as pltpu
from jax.sharding import PartitionSpec as P

MESH = pl.DeviceIdType.MESH
F32 = jnp.float32
BF16 = jnp.bfloat16


def split2(a):
    hi = a.astype(BF16)
    return hi, (a - hi.astype(F32)).astype(BF16)


def dot(a, b):
    return jnp.dot(a, b, preferred_element_type=F32)


TILE = 1024


class Place:
    def __init__(self, ng, nc):
        self.ng, self.nc, self.total, self.chips = ng, nc, ng * nc, ng // 2
        self.g = lax.axis_index("groups")
        self.i = lax.axis_index("grid")
        self.c = lax.axis_index("chol")
        self.core = lax.rem(self.i, 2)
        self.chip = lax.div(self.i, 2)
        self.sib = self.i + 1 - 2 * self.core
        self.flat = self.i * nc + self.c

    def peer(self, k):
        t = lax.rem(self.flat + k, self.total)
        return (self.g, lax.div(t, self.nc), lax.rem(t, self.nc))

    def greet(self):
        barrier = pltpu.get_barrier_semaphore()
        for k in range(1, self.total):
            pl.semaphore_signal(barrier, inc=1, device_id=self.peer(k), device_id_type=MESH)
        pl.semaphore_wait(barrier, self.total - 1)

    def send(self, src, dst, send_sem, recv_sem, to):
        return pltpu.make_async_remote_copy(
            src_ref=src, dst_ref=dst, send_sem=send_sem, recv_sem=recv_sem,
            device_id=(self.g, to, self.c), device_id_type=MESH)


def turn(xbuf, xt, xth, xtl):
    pts = xbuf.shape[0]
    tile = min(256, pts)

    @pl.loop(0, pts // tile)
    def _(p):
        at = pl.multiple_of(p * tile, tile)
        block = jnp.transpose(xbuf[pl.ds(at, tile), :])
        xt[:, pl.ds(at, tile)] = block
        hi, lo = split2(block)
        xth[:, pl.ds(at, tile)] = hi
        xtl[:, pl.ds(at, tile)] = lo


def add(acc, xt, xth, xtl, block, base, spans):
    count = block.shape[0]
    pts = xt.shape[1]
    tile = min(TILE, pts)
    hi, lo = split2(block)
    both = jnp.concatenate([hi, lo], axis=0)

    @pl.loop(0, pts // tile)
    def _(p):
        at = pl.multiple_of(p * tile, tile)
        cols = pl.ds(at, tile)
        half = None
        for first, where, width in spans:
            k = pl.ds(pl.multiple_of(where, 16), width)
            two = dot(both[:, first:first + width], xth[k, cols])
            term = two[:count] + (two[count:] + dot(hi[:, first:first + width], xtl[k, cols]))
            half = term if half is None else half + term
        prod = half * xt[pl.ds(pl.multiple_of(base, 8), count), cols]
        acc[:, cols] += jnp.sum(prod.reshape(count // 8, 8, tile), axis=0)


def finish(at, acc, allc, lhs_ref, rhs_ref, csend, crecv, drain):
    nc, pts = at.nc, allc.shape[2]
    allc[at.flat] = jnp.sum(acc[...], axis=0, keepdims=True)

    blocks = lhs_ref.shape[1] // pts
    mine = allc.at[at.flat]

    def push(slot, index, i, c):
        return pltpu.make_async_remote_copy(
            src_ref=mine, dst_ref=mine, send_sem=csend.at[slot], recv_sem=crecv.at[index],
            device_id=(at.g, i, c), device_id_type=MESH)

    def pull(j, n, index):
        theirs = allc.at[j * nc + n]
        return pltpu.make_async_remote_copy(
            src_ref=theirs, dst_ref=theirs, send_sem=csend.at[0], recv_sem=crecv.at[index],
            device_id=(at.g, at.i, at.c), device_id_type=MESH)

    first = blocks * nc
    home = lax.div(at.i, blocks)
    slot = lax.rem(at.i, blocks) * nc + at.c
    pushes = [push(k - 1, first + k - 1, at.i, lax.rem(at.c + k, nc)) for k in range(1, nc)]
    pushes += [push(nc - 1 + k - 1, slot, lax.rem(at.i + k, at.ng), home) for k in range(1, at.ng)]
    for copy in pushes:
        copy.start()
    lhs_ref[...] = jnp.zeros_like(lhs_ref)
    rhs_ref[...] = jnp.zeros_like(rhs_ref)
    drain()
    for k in range(1, nc):
        pull(at.i, lax.rem(at.c - k + nc, nc), first + k - 1).wait_recv()
    for b in range(blocks):
        j = at.c * blocks + b

        @pl.when(j != at.i)
        def _():
            for n in range(nc):
                pull(j, n, b * nc + n).wait_recv()

    def terms(v):
        h = v.astype(BF16).astype(F32)
        r = v - h
        m = r.astype(BF16).astype(F32)
        return h, m, (r - m).astype(BF16).astype(F32)

    for n in range(nc):
        h, m, l = terms(allc[at.i * nc + n])
        for t, v in enumerate((h, m, h, l, h, m)):
            rhs_ref[t * nc + n:t * nc + n + 1, :] = v
        for b in range(blocks):
            h, m, l = terms(allc[(at.c * blocks + b) * nc + n])
            for t, v in enumerate((h, h, m, h, l, m)):
                lhs_ref[t * nc + n:t * nc + n + 1, b * pts:(b + 1) * pts] = v
    for copy in pushes:
        copy.wait_send()


def begin(at, chol_hbm, orb_hbm, fit_hbm, held_ref, mine, xbuf, sems):
    copies = [pltpu.make_async_copy(chol_hbm.at[0], mine, sems.at[0]),
              pltpu.make_async_copy(orb_hbm, xbuf, sems.at[1]),
              pltpu.make_async_copy(fit_hbm, held_ref, sems.at[2])]
    copies[0].start()
    copies[1].start()
    at.greet()
    return copies


def pair_kernel(ng, nc, nch, chol_hbm, orb_hbm, fit_hbm, lhs_ref, rhs_ref, held_ref,
                lbuf, obuf, dsend, esend, dbuf, ebuf, xbuf, xt, xth, xtl, acc, allc,
                sems, ysend, yrecv, ssend, srecv, csend, crecv):
    at = Place(ng, nc)
    rows = lbuf.shape[1]
    half, step, wide = rows // 2, rows // nch, 2 * rows
    core, other = at.core, 1 - at.core
    away = (1 - at.chip) * 2 + core
    pieces = nch + 2
    own, xcopy, keep = begin(at, chol_hbm, orb_hbm, fit_hbm, held_ref, lbuf.at[core], xbuf, sems)
    far = pl.ds(pl.multiple_of((1 - at.chip) * wide, 128), wide)

    def slot(p, s):
        if p < nch:
            return obuf.at[s, pl.ds(p * step, step)]
        return (dbuf if p == nch else ebuf).at[s]

    def over(p):
        if p < nch:
            src = chol_hbm.at[0, pl.ds(p * step, step), far]
        else:
            src = dsend if p == nch else esend
        return at.send(src, slot(p, core), ysend.at[p], yrecv.at[p], away)

    def forward(p):
        return at.send(slot(p, core), slot(p, core), ssend.at[p], srecv.at[p], at.sib)

    for p in range(nch):
        over(p).start()
    home = at.send(chol_hbm.at[0], lbuf.at[core], ssend.at[pieces], srecv.at[pieces], at.sib)
    home.start()
    xcopy.wait()
    turn(xbuf, xt, xth, xtl)
    acc[...] = jnp.zeros_like(acc)

    own.wait()
    home.wait_recv()
    mine = pl.multiple_of(at.i * rows, 128)
    theirs = pl.multiple_of(at.sib * rows, 128)

    def both_ways(h):
        k = core + h - 2 * core * h
        one = lbuf[core, h * half:(h + 1) * half, pl.ds(pl.multiple_of(theirs + k * half, 128), half)]
        two = lbuf[other, pl.ds(pl.multiple_of(k * half, 8), half), pl.ds(pl.multiple_of(mine + h * half, 128), half)]
        return one + jnp.transpose(two)

    left = pl.ds(mine, half)
    right = pl.ds(pl.multiple_of(mine + half, 128), half)
    dsend[:, :half] = lbuf[core, :half, left]
    dsend[:, half:2 * half] = lbuf[core, :half, right] + jnp.transpose(lbuf[core, half:, left])
    dsend[:, 2 * half:] = both_ways(0)
    esend[:, :half] = lbuf[core, half:, right]
    esend[:, half:] = both_ways(1)
    over(nch).start()
    over(nch + 1).start()
    keep.start()

    put = functools.partial(add, acc, xt, xth, xtl)
    norb = lbuf.shape[2]
    put(lbuf[core], mine, [(0, 0, norb)])
    put(lbuf[other], theirs, [(0, 0, norb)])

    def take(p, s):
        src = ((1 - at.chip) * 2 + s) * rows
        sib = ((1 - at.chip) * 2 + 1 - s) * rows
        if p < nch:
            put(obuf[s, p * step:(p + 1) * step], src + p * step, [(0, at.chip * wide, wide)])
        elif p == nch:
            put(dbuf[s], src, [(0, src, 2 * half), (2 * half, sib + s * half, half)])
        else:
            put(ebuf[s], src + half, [(0, src + half, half), (half, sib + (1 - s) * half, half)])

    for p in range(pieces):
        over(p).wait_recv()
        forward(p).start()
        take(p, core)
        forward(p).wait_recv()
        take(p, other)

    def drain():
        home.wait_send()
        for p in range(pieces):
            over(p).wait_send()
            forward(p).wait_send()
        keep.wait()

    finish(at, acc, allc, lhs_ref, rhs_ref, csend, crecv, drain)


def ring_kernel(ng, nc, nch, chol_hbm, orb_hbm, fit_hbm, lhs_ref, rhs_ref, held_ref,
                lbuf, xbuf, xt, xth, xtl, acc, allc,
                sems, ysend, yrecv, ssend, srecv, csend, crecv):
    at = Place(ng, nc)
    rows, norb = lbuf.shape[1:]
    step = rows // nch
    own, xcopy, keep = begin(at, chol_hbm, orb_hbm, fit_hbm, held_ref, lbuf.at[at.i], xbuf, sems)

    def over(ch, d):
        part = pl.ds(ch * step, step)
        to = lax.rem(at.chip + d, at.chips) * 2 + at.core
        return at.send(chol_hbm.at[0, part], lbuf.at[at.i, part], ysend.at[ch, d], yrecv.at[ch, d], to)

    def source(d):
        return lax.rem(at.chip - d + at.chips, at.chips) * 2 + at.core

    def forward(ch, d):
        ref = lbuf.at[source(d), pl.ds(ch * step, step)]
        return at.send(ref, ref, ssend.at[ch, d], srecv.at[ch, d], at.sib)

    for ch in range(nch):
        for d in range(1, at.chips):
            over(ch, d).start()
    home = at.send(chol_hbm.at[0], lbuf.at[at.i], ssend.at[0, 0], srecv.at[0, 0], at.sib)
    home.start()
    keep.start()
    xcopy.wait()
    turn(xbuf, xt, xth, xtl)
    acc[...] = jnp.zeros_like(acc)

    def put(src, first, count):
        add(acc, xt, xth, xtl, lbuf[src, pl.ds(first, count), :], src * rows + first, [(0, 0, norb)])

    own.wait()
    put(at.i, 0, rows)
    home.wait()
    put(at.sib, 0, rows)
    for ch in range(nch):
        for d in range(1, at.chips):
            src = source(d)
            over(ch, d).wait_recv()
            forward(ch, d).start()
            put(src, ch * step, step)
            forward(ch, d).wait_recv()
            put(src + 1 - 2 * at.core, ch * step, step)

    def drain():
        for ch in range(nch):
            for d in range(1, at.chips):
                over(ch, d).wait_send()
                forward(ch, d).wait_send()
        keep.wait()

    finish(at, acc, allc, lhs_ref, rhs_ref, csend, crecv, drain)


def fit_kernel(pieces, lhs_ref, rhs_ref, held_ref, out_hbm, obuf, sems):
    left = jnp.transpose(lhs_ref[...]).astype(BF16)
    right = rhs_ref[...].astype(BF16)
    step = obuf.shape[0] // pieces
    copies = []
    for p in range(pieces):
        part = pl.ds(p * step, step)
        obuf[part, :] = held_ref[part, :] + dot(left[p * step:(p + 1) * step], right)
        copies.append(pltpu.make_async_copy(obuf.at[part], out_hbm.at[part], sems.at[p]))
        copies[-1].start()
    for copy in copies:
        copy.wait()


def on_device(ng, nc, chol_block, orbitals, fit_in):
    rows, norb = chol_block.shape[1:]
    pts = orbitals.shape[0]
    tile_rows, tile_cols = fit_in.shape
    chips = ng // 2
    depth = -(-6 * nc // 8) * 8
    total = ng * nc
    dma = pltpu.SemaphoreType.DMA
    vmem = pl.BlockSpec(memory_space=pltpu.VMEM)
    hbm = pl.BlockSpec(memory_space=pltpu.HBM)
    if chips == 2 and rows % 256 == 0:
        kernel, nch, half = pair_kernel, 2, rows // 2
        blocks = [(2, rows, norb), (2, rows, 2 * rows), (half, 3 * half), (half, 2 * half),
                  (2, half, 3 * half), (2, half, 2 * half)]
        links = [dma((nch + 2,)), dma((nch + 2,)), dma((nch + 3,)), dma((nch + 3,))]
    else:
        kernel, nch = ring_kernel, 4
        blocks = [(ng, rows, norb)]
        links = [dma((nch, chips))] * 4
    lhs, rhs, held = pl.pallas_call(
        functools.partial(kernel, ng, nc, nch),
        out_shape=(jax.ShapeDtypeStruct((depth, tile_rows), F32),
                   jax.ShapeDtypeStruct((depth, tile_cols), F32),
                   jax.ShapeDtypeStruct(fit_in.shape, F32)),
        in_specs=[hbm, hbm, hbm],
        out_specs=(vmem, vmem, vmem),
        scratch_shapes=[
            *(pltpu.VMEM(shape, F32) for shape in blocks),
            pltpu.VMEM((pts, norb), F32),
            pltpu.VMEM((norb, pts), F32),
            pltpu.VMEM((norb, pts), BF16),
            pltpu.VMEM((norb, pts), BF16),
            pltpu.VMEM((8, pts), F32),
            pltpu.VMEM((total, 1, pts), F32),
            dma((3,)), *links,
            dma((ng + nc,)), dma(((tile_rows // pts + 1) * nc,)),
        ],
        compiler_params=pltpu.CompilerParams(
            collective_id=0, has_side_effects=True, vmem_limit_bytes=40 << 20),
        name="gather",
    )(*(pltpu.with_memory_space_constraint(a, pltpu.HBM) for a in (chol_block, orbitals, fit_in)))
    pieces = 8
    return pl.pallas_call(
        functools.partial(fit_kernel, pieces),
        out_shape=jax.ShapeDtypeStruct(fit_in.shape, F32),
        in_specs=[vmem, vmem, vmem],
        out_specs=hbm,
        scratch_shapes=[pltpu.VMEM(fit_in.shape, F32), dma((pieces,))],
        compiler_params=pltpu.CompilerParams(vmem_limit_bytes=20 << 20),
        name="fit",
    )(lhs, rhs, held)


def solution(mesh):
    placed = (
        P(("groups", "chol"), "grid", None),
        P(("groups", "grid"), None),
        P(("groups", "chol"), "grid"),
    )
    return jax.shard_map(
        functools.partial(on_device, mesh.shape["grid"], mesh.shape["chol"]),
        mesh=mesh,
        in_specs=placed,
        out_specs=P(("groups", "chol"), "grid"),
        check_vma=False,
    )
```
